32 devices in a mesh: vel: 4 (over y, x), space: 8 (over z, core).
Axes of the slice: x: 2, y: 2, z: 4, core: 2. Of those that a mesh axis runs over, the one named last changes fastest.
Arguments:
- density: float32 [1024, 32, 8, 128], P('vel', 'space'), may hold values from -6 to 6
- limiter: int32 [32, 8, 128], P('space'), may hold values from 0 to 2
- heading: int32 [1024], P('vel'), may hold values from 0 to 1
- courant: float32 [1024], P('vel'), may hold values from 0.1 to 0.9
- kernel_slices: bfloat16 [16, 1024, 1024], P('space', None, 'vel'), may hold values from -0.046875 to 0.046875
Outputs:
- transported: float32 [1024, 32, 8, 128], P('vel', 'space')
- collision: float32 [1024, 32, 8, 128], P('vel', 'space')
The draws below stay inside these ranges and needn't reach their ends.
Inputs may be any that keep to these rules, and one draw needn't show every extreme that they name: `limiter`: 0 no slope, 1 minmod slope, 2 central slope.
All inputs are finite; a program needn't handle non-finite values.
Results may differ from the reference program's by a relative error of at most 0.0041.
Values may be sent and summed in bfloat16 or wider, within the bound.
A program may use at most 128 MiB of HBM per device.

```python
import math
import jax
import jax.numpy as jnp
from jax import lax

V = 1024
SLICES = 16
NY = 8
NZ = 128
NX = 32


def touch_ends(result, key, smallest, high):
    shape = result.shape
    spot = [jax.random.randint(jax.random.fold_in(key, axis), (), 0, shape[axis]) for axis in range(len(shape))]
    result = result.at[tuple(spot)].set(smallest)
    longest = shape.index(max(shape))
    spot[longest] = (spot[longest] + 1) % shape[longest]
    return result.at[tuple(spot)].set(high)


def levels(stream_key, shape, split, smallest, top_value):
    loudness = 1.0
    for dim, blocks in split:
        heights = jax.random.uniform(jax.random.fold_in(jax.random.fold_in(stream_key, 6), dim), (blocks,), jnp.float32, smallest / len(split), top_value / len(split))
        loudness = loudness * jnp.repeat(jnp.exp(heights), shape[dim] // blocks).reshape((-1,) + (1,) * (len(shape) - 1 - dim))
    return loudness


def scatter_about(key, shape, scale, limit, split=(), kind=jnp.bfloat16):
    factor_of = levels(key, shape, split, -0.22, 0.18) if split else 1.0
    values = jax.random.normal(key, shape, jnp.float32) * scale * factor_of
    return jnp.minimum(jnp.maximum(values, -limit), limit).astype(kind)


def setup_inputs(seed: int = 0) -> dict:
    key_list = jax.random.split(jax.random.key(seed), 6)
    density = scatter_about(key_list[0], (V, NX, NY, NZ), 1.0, 6.0, ((0, 4), (1, 8)), jnp.float32)
    limiter = touch_ends(jax.random.randint(key_list[1], (NX, NY, NZ), 0, 3), jax.random.fold_in(key_list[1], 1), 0, 2).astype(jnp.int32)
    heading = touch_ends(jax.random.randint(key_list[2], (V,), 0, 2), jax.random.fold_in(key_list[2], 1), 0, 1).astype(jnp.int32)
    courant = jnp.clip(jnp.exp(math.log(0.9) - 2.1972245 * jax.random.uniform(key_list[3], (V,), jnp.float32) ** levels(key_list[3], (V,), ((0, 4),), -0.2, 0.2)), 0.1, 0.9)
    kernel_slices = scatter_about(key_list[4], (SLICES, V, V), (V * SLICES) ** -0.5, 0.046875, ((0, 8), (2, 4)))
    return dict(density=density, limiter=limiter, heading=heading, courant=courant, kernel_slices=kernel_slices)


def limited_slopes(left_diff, right_diff, limiter):
    minmod_slope = jnp.where(left_diff * right_diff > 0, jnp.sign(left_diff) * jnp.minimum(jnp.abs(left_diff), jnp.abs(right_diff)), jnp.zeros_like(left_diff))
    central = 0.5 * (left_diff + right_diff)
    codes = limiter[None]
    return jnp.where(codes == 1, minmod_slope, jnp.where(codes == 2, central, jnp.zeros_like(central)))


def reference(density, limiter, heading, courant, kernel_slices):
    layers = ((0, 0), (1, 1), (0, 0), (0, 0))
    padded = jnp.pad(density, layers)
    left_diff = density - padded[:, :-2]
    right_diff = padded[:, 2:] - density
    slopes = limited_slopes(left_diff, right_diff, limiter)
    upwind = (2 * heading - 1).astype(density.dtype)[:, None, None, None]
    rebuilt = density + 0.5 * upwind * slopes
    rebuilt_pad = jnp.pad(rebuilt, layers)
    forward = (heading == 1)[:, None, None, None]
    upstream = jnp.where(forward, rebuilt_pad[:, :-2], rebuilt_pad[:, 2:])
    transported = density - courant[:, None, None, None] * (rebuilt - upstream)
    moved = transported.astype(jnp.bfloat16).reshape(V, -1)
    stride = V // SLICES

    def apply_one(running, position):
        matrix = kernel_slices[position]
        projected = jnp.dot(matrix.T, moved, preferred_element_type=jnp.float32)
        weight = moved[position * stride].astype(jnp.float32)
        return running + weight[None, :] * projected, position

    initial = jnp.zeros(moved.shape, jnp.float32)
    collision = lax.scan(apply_one, initial, jnp.arange(SLICES, dtype=jnp.int32))[0]
    return transported, collision.reshape(density.shape)
```

```python
import functools

import jax
import jax.numpy as jnp
from jax import lax
from jax.experimental import pallas as pl
from jax.experimental.pallas import tpu as pltpu
from jax.sharding import PartitionSpec as P

MESH = pl.DeviceIdType.MESH
HOP_STEPS = (4, 6)


def minmod(left, right):
    small = jnp.where(left > 0, jnp.minimum(left, right), jnp.maximum(left, right))
    return jnp.where(left * right > 0, small, jnp.zeros_like(left))


def kernel(
    nv, ns, nx, ny, vl, nsl,
    dens_ref, lim_ref, vel_ref, ker_ref,
    trans_ref, coll_ref,
    acc, gath, kt, send_up, send_dn, recv_lo, recv_hi, lim_lo, lim_hi,
    halo_s, halo_r, lim_s, lim_r, v1_s, v1_r, v2_s, v2_r, k_s, k_r, c_s, c_r,
):
    vels = nv * vl
    lanes = dens_ref.shape[1]
    stride = vels // (nsl * ns)
    half = vl // 2
    v = lax.axis_index("vel")
    sp = lax.axis_index("space")
    nz = ns // 2
    z = sp // 2
    core = sp % 2
    relay = nv == 4
    if relay:
        partners = [v + 1 - 2 * (v % 2), v + 2 - 4 * ((v // 2) % 2)]
        sources = partners
    else:
        partners = [(v + p) % nv for p in range(1, nv)]
        sources = [(v + nv - p) % nv for p in range(1, nv)]
    sibling = 2 * z + 1 - core
    z_up = 2 * ((z + 1) % nz) + core
    z_dn = 2 * ((z + nz - 1) % nz) + core
    s_up = (sp + 1) % ns
    s_dn = (sp + ns - 1) % ns
    has_lo = sp > 0
    has_hi = sp < ns - 1

    barrier = pltpu.get_barrier_semaphore()
    for p in partners:
        pl.semaphore_signal(barrier, inc=1, device_id={"vel": p}, device_id_type=MESH)
    for p in (sibling, z_up, z_dn, s_up, s_dn):
        pl.semaphore_signal(barrier, inc=1, device_id={"space": p}, device_id_type=MESH)
    pl.semaphore_wait(barrier, len(partners) + 5)

    def remote(src, dst, ss, rs, axis, peer):
        return pltpu.make_async_remote_copy(
            src_ref=src, dst_ref=dst, send_sem=ss, recv_sem=rs,
            device_id={axis: peer}, device_id_type=MESH,
        )

    def halo_up(y):
        return remote(send_up.at[y], recv_lo.at[y], halo_s.at[0, y], halo_r.at[0, y], "space", s_up)

    def halo_dn(y):
        return remote(send_dn.at[y], recv_hi.at[y], halo_s.at[1, y], halo_r.at[1, y], "space", s_dn)

    lim_up = remote(lim_ref.at[pl.ds((nx - 1) * ny, ny)], lim_lo, lim_s.at[0], lim_r.at[0], "space", s_up)
    lim_dn = remote(lim_ref.at[pl.ds(0, ny)], lim_hi, lim_s.at[1], lim_r.at[1], "space", s_dn)

    @pl.when(has_hi)
    def _():
        lim_up.start()

    @pl.when(has_lo)
    def _():
        lim_dn.start()

    rows = nx * ny

    def cells(x, y, start, size):
        return dens_ref[pl.ds(start * rows + x * ny + y, size, stride=rows), :]

    @pl.loop(0, ny)
    def _(y):
        send_up[y, 0] = cells(nx - 1, y, 0, vl).astype(jnp.bfloat16)
        send_up[y, 1] = cells(nx - 2, y, 0, vl).astype(jnp.bfloat16)
        send_dn[y, 0] = cells(0, y, 0, vl).astype(jnp.bfloat16)
        send_dn[y, 1] = cells(1, y, 0, vl).astype(jnp.bfloat16)

        @pl.when(has_hi)
        def _():
            halo_up(y).start()

        @pl.when(has_lo)
        def _():
            halo_dn(y).start()

    def block(shard):
        return kt.at[pl.ds(shard * nsl, nsl)]

    blk = min(256, vels)

    @pl.loop(0, nsl)
    def _(i):
        for j in range(0, vels, blk):
            kt[sp * nsl + i, :, j : j + blk] = ker_ref[i, j : j + blk, :].T

    hops = nz // 2

    def k_piece(chip, hop, up):
        shard = 2 * chip + core
        if nz % 2 == 0 and hop == hops:
            first = 0 if up else half
            return kt.at[pl.ds(shard * nsl, nsl), pl.ds(first, half)]
        return block(shard)

    def k_hop(hop, up):
        if up:
            piece = k_piece((z + nz - (hop - 1)) % nz, hop, True)
            return remote(piece, piece, k_s.at[0, hop - 1], k_r.at[0, hop - 1], "space", z_up)
        piece = k_piece((z + hop - 1) % nz, hop, False)
        return remote(piece, piece, k_s.at[1, hop - 1], k_r.at[1, hop - 1], "space", z_dn)

    def k_arrival(hop, up):
        if up:
            piece = k_piece((z + nz - hop) % nz, hop, True)
            return remote(piece, piece, k_s.at[0, hop - 1], k_r.at[0, hop - 1], "space", z_up)
        piece = k_piece((z + hop) % nz, hop, False)
        return remote(piece, piece, k_s.at[1, hop - 1], k_r.at[1, hop - 1], "space", z_dn)

    def chip_of(n):
        if n == 0:
            return z
        d = (n + 1) // 2
        return (z + d) % nz if n % 2 else (z + nz - d) % nz

    def across(n):
        piece = block(2 * chip_of(n) + core)
        return remote(piece, piece, c_s.at[n], c_r.at[n], "space", sibling)

    def from_sibling(n):
        piece = block(2 * chip_of(n) + 1 - core)
        return remote(piece, piece, c_s.at[n], c_r.at[n], "space", sibling)

    if hops:
        k_hop(1, True).start()
        k_hop(1, False).start()
    across(0).start()

    @pl.when(has_lo)
    def _():
        lim_up.wait_recv()

    @pl.when(has_hi)
    def _():
        lim_dn.wait_recv()

    @pl.when(jnp.logical_not(has_lo))
    def _():
        lim_lo[...] = jnp.zeros_like(lim_lo)
        recv_lo[...] = jnp.zeros_like(recv_lo)

    @pl.when(jnp.logical_not(has_hi))
    def _():
        lim_hi[...] = jnp.zeros_like(lim_hi)
        recv_hi[...] = jnp.zeros_like(recv_hi)

    def slope(left, right, code):
        central = 0.5 * (left + right)
        return jnp.where(
            code == 1, minmod(left, right), jnp.where(code == 2, central, jnp.zeros_like(central))
        )

    rb = 32

    def transport(y):
        @pl.loop(0, vl // rb)
        def _(b):
            r0 = pl.multiple_of(b * rb, rb)
            signed = vel_ref[pl.ds(r0, rb), :]
            forward = signed > 0
            cour = jnp.abs(signed)
            upw = jnp.where(forward, jnp.float32(0.5), jnp.float32(-0.5))
            d = [recv_lo[y, 1, pl.ds(r0, rb), :].astype(jnp.float32),
                 recv_lo[y, 0, pl.ds(r0, rb), :].astype(jnp.float32)]
            d += [cells(x, y, r0, rb) for x in range(nx)]
            d += [recv_hi[y, 0, pl.ds(r0, rb), :].astype(jnp.float32),
                  recv_hi[y, 1, pl.ds(r0, rb), :].astype(jnp.float32)]
            codes = [lim_lo[pl.ds(y, 1), :]]
            codes += [lim_ref[pl.ds(x * ny + y, 1), :] for x in range(nx)]
            codes += [lim_hi[pl.ds(y, 1), :]]
            diff = [d[i + 1] - d[i] for i in range(nx + 3)]
            r = []
            for i in range(nx + 2):
                code = jnp.broadcast_to(codes[i], (rb, lanes))
                r.append(d[i + 1] + upw * slope(diff[i], diff[i + 1], code))
            for x in range(nx):
                upstream = jnp.where(forward, r[x], r[x + 2])
                out = d[x + 2] - cour * (r[x + 1] - upstream)
                trans_ref[pl.ds(r0 * rows + x * ny + y, rb, stride=rows), :] = out
                gath[y, pl.ds(pl.multiple_of(v * vl + r0, rb), rb), x * lanes : (x + 1) * lanes] = (
                    out.astype(jnp.bfloat16)
                )

    def mine(y, owner):
        return gath.at[y, pl.ds(pl.multiple_of(owner * vl, vl), vl)]

    def first_phase(y, p):
        return remote(mine(y, v), mine(y, v), v1_s.at[p, y], v1_r.at[p, y], "vel", partners[p])

    def first_arrival(y, p):
        piece = mine(y, sources[p])
        return remote(piece, piece, v1_s.at[p, y], v1_r.at[p, y], "vel", partners[p])

    def part(y, owner, which):
        return gath.at[y, pl.ds(pl.multiple_of(owner * vl + which * half, half), half)]

    def second_phase(y, p):
        piece = part(y, partners[1 - p], p)
        return remote(piece, piece, v2_s.at[p, y], v2_r.at[p, y], "vel", partners[p])

    def second_arrival(y, p):
        far = partners[0] + partners[1] - v
        piece = part(y, far, p)
        return remote(piece, piece, v2_s.at[p, y], v2_r.at[p, y], "vel", partners[p])

    def one(c, shard):
        total = acc[c]
        for i in range(nsl):
            s = shard * nsl + i
            prod = jnp.dot(kt[s], gath[c], preferred_element_type=jnp.float32)
            row = gath[c, pl.ds(pl.multiple_of(s * stride, stride), 1), :].astype(jnp.float32)
            total = total + row * prod
        acc[c] = total

    def shard_at(n):
        k = n // 2
        odd = k % 2
        d = (k + 1) // 2
        chip = (z + odd * d + (1 - odd) * (nz - d)) % nz
        return 2 * chip + (core + n % 2) % 2

    at_one = min(HOP_STEPS[0], ny - 1)
    at_far = min(HOP_STEPS[1], ny - 1)
    n_near = min(3, nz)

    def compute(c, first, last, start):
        early = jnp.where(c < start, c + 1, jnp.where(c == start, 0, c))

        @pl.loop(early, c + 1)
        def _(cc):
            @pl.loop(first, last)
            def _(n):
                one(cc, shard_at(n))

    acc[...] = jnp.zeros_like(acc)

    @pl.loop(0, ny + 2)
    def _(t):
        @pl.when(t < ny)
        def _():
            @pl.when(has_lo)
            def _():
                halo_up(t).wait_recv()

            @pl.when(has_hi)
            def _():
                halo_dn(t).wait_recv()

            transport(t)
            for p in range(len(partners)):
                first_phase(t, p).start()

        @pl.when(jnp.logical_and(t >= 1, t < ny + 1))
        def _():
            for p in range(len(partners)):
                first_arrival(t - 1, p).wait_recv()
            if relay:
                for p in range(2):
                    second_phase(t - 1, p).start()

        @pl.when(t == at_one + 1)
        def _():
            if hops:
                for up in (True, False):
                    k_arrival(1, up).wait_recv()
                if hops > 1:
                    for up in (True, False):
                        k_hop(2, up).start()
                for n in range(1, n_near):
                    across(n).start()

        @pl.when(t == at_far + 1)
        def _():
            for hop in range(2, hops + 1):
                for up in (True, False):
                    k_arrival(hop, up).wait_recv()
                if hop < hops:
                    for up in (True, False):
                        k_hop(hop + 1, up).start()
            for n in range(n_near, nz):
                across(n).start()

        @pl.when(t == 2)
        def _():
            from_sibling(0).wait_recv()

        @pl.when(t >= 2)
        def _():
            c = t - 2
            if relay:
                for p in range(2):
                    second_arrival(c, p).wait_recv()
            compute(c, 0, 2, 0)

            @pl.when(c == at_one)
            def _():
                for n in range(1, n_near):
                    from_sibling(n).wait_recv()

            compute(c, 2, 2 * n_near, at_one)

            @pl.when(c == at_far)
            def _():
                for n in range(n_near, nz):
                    from_sibling(n).wait_recv()

            compute(c, 2 * n_near, ns, at_far)

    @pl.loop(0, ny)
    def _(y):
        for x in range(nx):
            coll_ref[pl.ds(x * ny + y, vl, stride=rows), :] = acc[y, :, x * lanes : (x + 1) * lanes]

        @pl.when(has_hi)
        def _():
            halo_up(y).wait_send()

        @pl.when(has_lo)
        def _():
            halo_dn(y).wait_send()

        for p in range(len(partners)):
            first_phase(y, p).wait_send()
        if relay:
            for p in range(2):
                second_phase(y, p).wait_send()

    @pl.when(has_hi)
    def _():
        lim_up.wait_send()

    @pl.when(has_lo)
    def _():
        lim_dn.wait_send()

    for hop in range(1, hops + 1):
        for up in (True, False):
            k_hop(hop, up).wait_send()
    for n in range(nz):
        across(n).wait_send()


def local(nv, ns, density, limiter, heading, courant, kernel_slices):
    vl, nx, ny, lanes = density.shape
    nsl, vels, _ = kernel_slices.shape
    rows = nx * ny
    nz = ns // 2
    bf16, f32 = jnp.bfloat16, jnp.float32
    dens = density.reshape(vl * rows, lanes)
    lim = limiter.reshape(rows, lanes)
    signed = jnp.where(heading == 1, courant, -courant)
    signed = jnp.broadcast_to(signed[:, None], (vl, lanes))
    dma = pltpu.SemaphoreType.DMA
    n_part = 2 if nv == 4 else max(nv - 1, 1)
    vmem = pl.BlockSpec(memory_space=pltpu.VMEM)
    out = jax.ShapeDtypeStruct(dens.shape, f32)
    hops = max(nz // 2, 1)
    trans, coll = pl.pallas_call(
        functools.partial(kernel, nv, ns, nx, ny, vl, nsl),
        out_shape=(out, out),
        in_specs=[vmem] * 4,
        out_specs=(vmem, vmem),
        scratch_shapes=[
            pltpu.VMEM((ny, vl, nx * lanes), f32),
            pltpu.VMEM((ny, vels, nx * lanes), bf16),
            pltpu.VMEM((nsl * ns, vl, vels), bf16),
            pltpu.VMEM((ny, 2, vl, lanes), bf16),
            pltpu.VMEM((ny, 2, vl, lanes), bf16),
            pltpu.VMEM((ny, 2, vl, lanes), bf16),
            pltpu.VMEM((ny, 2, vl, lanes), bf16),
            pltpu.VMEM((ny, lanes), jnp.int32),
            pltpu.VMEM((ny, lanes), jnp.int32),
            dma((2, ny)), dma((2, ny)), dma((2,)), dma((2,)),
            dma((n_part, ny)), dma((n_part, ny)), dma((2, ny)), dma((2, ny)),
            dma((2, hops)), dma((2, hops)), dma((nz,)), dma((nz,)),
        ],
        compiler_params=pltpu.CompilerParams(
            collective_id=0, has_side_effects=True, vmem_limit_bytes=60 * 1024 * 1024
        ),
    )(dens, lim, signed, kernel_slices)
    return trans.reshape(density.shape), coll.reshape(density.shape)


def solution(mesh):
    return jax.shard_map(
        functools.partial(local, mesh.shape["vel"], mesh.shape["space"]),
        mesh=mesh,
        in_specs=(
            P("vel", "space", None, None),
            P("space", None, None),
            P("vel"),
            P("vel"),
            P("space", None, "vel"),
        ),
        out_specs=(P("vel", "space", None, None), P("vel", "space", None, None)),
        check_vma=False,
    )
```

```python
import functools

import jax
import jax.numpy as jnp
from jax import lax
from jax.experimental import pallas as pl
from jax.experimental.pallas import tpu as pltpu
from jax.sharding import PartitionSpec as P

MESH = pl.DeviceIdType.MESH


def minmod(left, right):
    small = jnp.where(left > 0, jnp.minimum(left, right), jnp.maximum(left, right))
    return jnp.where(left * right > 0, small, jnp.zeros_like(left))


def kernel(
    nv, ns, nx, ny, vl, nsl,
    dens_ref, lim_ref, vel_ref, ker_ref,
    trans_ref, coll_ref,
    acc, gath, kt, send_up, send_dn, recv_lo, recv_hi, lim_lo, lim_hi,
    dbuf, in_s, trans_s, coll_s,
    halo_s, halo_r, lim_s, lim_r, v1_s, v1_r, v2_s, v2_r, k_s, k_r, c_s, c_r,
):
    vels = nv * vl
    lanes = dens_ref.shape[3]
    stride = vels // (nsl * ns)
    half = vl // 2
    v = lax.axis_index("vel")
    sp = lax.axis_index("space")
    nz = ns // 2
    z = sp // 2
    core = sp % 2
    relay = nv == 4
    if relay:
        partners = [v + 1 - 2 * (v % 2), v + 2 - 4 * ((v // 2) % 2)]
        sources = partners
    else:
        partners = [(v + p) % nv for p in range(1, nv)]
        sources = [(v + nv - p) % nv for p in range(1, nv)]
    sibling = 2 * z + 1 - core
    z_up = 2 * ((z + 1) % nz) + core
    z_dn = 2 * ((z + nz - 1) % nz) + core
    s_up = (sp + 1) % ns
    s_dn = (sp + ns - 1) % ns
    has_lo = sp > 0
    has_hi = sp < ns - 1
    groups = nz * nsl

    def load(x, y):
        return pltpu.make_async_copy(dens_ref.at[:, x * ny + y, 0, :], dbuf.at[y, x], in_s.at[y, x])

    def save(x, y):
        return pltpu.make_async_copy(dbuf.at[y, x], trans_ref.at[:, x * ny + y, 0, :], trans_s.at[y, x])

    def give(x, y):
        tile = acc.at[y, :, pl.ds(x * lanes, lanes)]
        return pltpu.make_async_copy(tile, coll_ref.at[:, x * ny + y, 0, :], coll_s.at[y, x])

    @pl.loop(0, ny)
    def _(y):
        for x in range(nx):
            load(x, y).start()

    barrier = pltpu.get_barrier_semaphore()
    for p in partners:
        pl.semaphore_signal(barrier, inc=1, device_id={"vel": p}, device_id_type=MESH)
    for p in (sibling, z_up, z_dn, s_up, s_dn):
        pl.semaphore_signal(barrier, inc=1, device_id={"space": p}, device_id_type=MESH)
    pl.semaphore_wait(barrier, len(partners) + 5)

    def remote(src, dst, ss, rs, axis, peer):
        return pltpu.make_async_remote_copy(
            src_ref=src, dst_ref=dst, send_sem=ss, recv_sem=rs,
            device_id={axis: peer}, device_id_type=MESH,
        )

    def halo_up(y):
        return remote(send_up.at[y], recv_lo.at[y], halo_s.at[0, y], halo_r.at[0, y], "space", s_up)

    def halo_dn(y):
        return remote(send_dn.at[y], recv_hi.at[y], halo_s.at[1, y], halo_r.at[1, y], "space", s_dn)

    lim_up = remote(lim_ref.at[pl.ds((nx - 1) * ny, ny)], lim_lo, lim_s.at[0], lim_r.at[0], "space", s_up)
    lim_dn = remote(lim_ref.at[pl.ds(0, ny)], lim_hi, lim_s.at[1], lim_r.at[1], "space", s_dn)

    @pl.when(has_hi)
    def _():
        lim_up.start()

    @pl.when(has_lo)
    def _():
        lim_dn.start()

    blk = min(256, vels)

    def chip_at(way, h):
        return z - h if way == 0 else z + h

    def held(way, h):
        return z - h >= 0 if way == 0 else z + h < nz

    def slice_of(way, h, i, c):
        return kt.at[pl.ds((2 * chip_at(way, h) + c) * nsl + i, 1)]

    def onward(way, h, i):
        piece = slice_of(way, h, i, core)
        return remote(piece, piece, k_s.at[way, h, i], k_r.at[way, h, i], "space", (z_up, z_dn)[way])

    def sends(way, h):
        more = z < nz - 1 if way == 0 else z > 0
        return jnp.logical_and(more, held(way, h))

    def arrival(way, h, i):
        piece = slice_of(way, h, i, core)
        return remote(piece, piece, k_s.at[way, h - 1, i], k_r.at[way, h - 1, i], "space", (z_up, z_dn)[way])

    def across(way, h, i):
        piece = slice_of(way, h, i, core)
        return remote(piece, piece, c_s.at[way, h, i], c_r.at[way, h, i], "space", sibling)

    def from_sibling(way, h, i):
        piece = slice_of(way, h, i, 1 - core)
        return remote(piece, piece, c_s.at[way, h, i], c_r.at[way, h, i], "space", sibling)

    @pl.loop(0, nsl)
    def _(i):
        for j in range(0, vels, blk):
            kt[sp * nsl + i, :, j : j + blk] = ker_ref[i, j : j + blk, :].T
        for way in range(2):
            @pl.when(sends(way, 0))
            def _():
                onward(way, 0, i).start()
        across(0, 0, i).start()

    @pl.loop(0, ny)
    def _(y):
        for x in range(nx):
            load(x, y).wait()
        send_up[y, 0] = dbuf[y, nx - 1].astype(jnp.bfloat16)
        send_up[y, 1] = dbuf[y, nx - 2].astype(jnp.bfloat16)
        send_dn[y, 0] = dbuf[y, 0].astype(jnp.bfloat16)
        send_dn[y, 1] = dbuf[y, 1].astype(jnp.bfloat16)

        @pl.when(has_hi)
        def _():
            halo_up(y).start()

        @pl.when(has_lo)
        def _():
            halo_dn(y).start()

    @pl.when(has_lo)
    def _():
        lim_up.wait_recv()

    @pl.when(has_hi)
    def _():
        lim_dn.wait_recv()

    @pl.when(jnp.logical_not(has_lo))
    def _():
        lim_lo[...] = jnp.zeros_like(lim_lo)
        recv_lo[...] = jnp.zeros_like(recv_lo)

    @pl.when(jnp.logical_not(has_hi))
    def _():
        lim_hi[...] = jnp.zeros_like(lim_hi)
        recv_hi[...] = jnp.zeros_like(recv_hi)

    def slope(left, right, code):
        central = 0.5 * (left + right)
        return jnp.where(
            code == 1, minmod(left, right), jnp.where(code == 2, central, jnp.zeros_like(central))
        )

    rb = 32

    def transport(y):
        @pl.loop(0, vl // rb)
        def _(b):
            r0 = pl.multiple_of(b * rb, rb)
            signed = vel_ref[pl.ds(r0, rb), :]
            forward = signed > 0
            cour = jnp.abs(signed)
            upw = jnp.where(forward, jnp.float32(0.5), jnp.float32(-0.5))
            d = [recv_lo[y, 1, pl.ds(r0, rb), :].astype(jnp.float32),
                 recv_lo[y, 0, pl.ds(r0, rb), :].astype(jnp.float32)]
            d += [dbuf[y, x, pl.ds(r0, rb), :] for x in range(nx)]
            d += [recv_hi[y, 0, pl.ds(r0, rb), :].astype(jnp.float32),
                  recv_hi[y, 1, pl.ds(r0, rb), :].astype(jnp.float32)]
            codes = [lim_lo[pl.ds(y, 1), :]]
            codes += [lim_ref[pl.ds(x * ny + y, 1), :] for x in range(nx)]
            codes += [lim_hi[pl.ds(y, 1), :]]
            diff = [d[i + 1] - d[i] for i in range(nx + 3)]
            r = []
            for i in range(nx + 2):
                code = jnp.broadcast_to(codes[i], (rb, lanes))
                r.append(d[i + 1] + upw * slope(diff[i], diff[i + 1], code))
            for x in range(nx):
                upstream = jnp.where(forward, r[x], r[x + 2])
                out = d[x + 2] - cour * (r[x + 1] - upstream)
                dbuf[y, x, pl.ds(r0, rb), :] = out
                gath[y, pl.ds(pl.multiple_of(v * vl + r0, rb), rb), x * lanes : (x + 1) * lanes] = (
                    out.astype(jnp.bfloat16)
                )

    def mine(y, owner):
        return gath.at[y, pl.ds(pl.multiple_of(owner * vl, vl), vl)]

    def first_phase(y, p):
        return remote(mine(y, v), mine(y, v), v1_s.at[p, y], v1_r.at[p, y], "vel", partners[p])

    def first_arrival(y, p):
        piece = mine(y, sources[p])
        return remote(piece, piece, v1_s.at[p, y], v1_r.at[p, y], "vel", partners[p])

    def part(y, owner, which):
        return gath.at[y, pl.ds(pl.multiple_of(owner * vl + which * half, half), half)]

    def second_phase(y, p):
        piece = part(y, partners[1 - p], p)
        return remote(piece, piece, v2_s.at[p, y], v2_r.at[p, y], "vel", partners[p])

    def second_arrival(y, p):
        far = partners[0] + partners[1] - v
        piece = part(y, far, p)
        return remote(piece, piece, v2_s.at[p, y], v2_r.at[p, y], "vel", partners[p])

    def one(c, chip, i):
        total = acc[c]
        for k in range(2):
            s = (2 * chip + k) * nsl + i
            prod = jnp.dot(kt[s], gath[c], preferred_element_type=jnp.float32)
            row = gath[c, pl.ds(pl.multiple_of(s * stride, stride), 1), :].astype(jnp.float32)
            total = total + row * prod
        acc[c] = total

    def first_chunk(g):
        later = jnp.clip(((g - 1) * ny) // groups, 1, ny - 1)
        return jnp.where(g < nsl, 0, later)

    def compute(c):
        @pl.loop(0, groups)
        def _(g):
            h, i = g // nsl, g % nsl
            start = first_chunk(g)
            early = jnp.where(c < start, c + 1, jnp.where(c == start, 0, c))
            for way in range(2):
                here = held(way, h) if way == 0 else jnp.logical_and(h > 0, held(way, h))

                @pl.when(jnp.logical_and(here, c == start))
                def _():
                    from_sibling(way, h, i).wait_recv()

            @pl.loop(early, c + 1)
            def _(cc):
                low = jnp.where(z - h >= 0, 0, 1)
                high = jnp.where(jnp.logical_and(h > 0, z + h < nz), 2, 1)

                @pl.loop(low, high)
                def _(way):
                    one(cc, z + (2 * way - 1) * h, i)

                @pl.when(jnp.logical_and(g == groups - 1, c >= start))
                def _():
                    for x in range(nx):
                        give(x, cc).start()

    def service(c):
        @pl.loop(nsl, groups)
        def _(g):
            h, i = g // nsl, g % nsl

            @pl.when(first_chunk(g) == c)
            def _():
                for way in range(2):
                    @pl.when(held(way, h))
                    def _():
                        arrival(way, h, i).wait_recv()

                        @pl.when(sends(way, h))
                        def _():
                            onward(way, h, i).start()

                        across(way, h, i).start()

    @pl.loop(0, ny + 2)
    def _(t):
        @pl.when(t < ny)
        def _():
            @pl.when(has_lo)
            def _():
                halo_up(t).wait_recv()

            @pl.when(has_hi)
            def _():
                halo_dn(t).wait_recv()

            transport(t)
            for p in range(len(partners)):
                first_phase(t, p).start()
            for x in range(nx):
                save(x, t).start()

        @pl.when(jnp.logical_and(t >= 1, t < ny + 1))
        def _():
            for p in range(len(partners)):
                first_arrival(t - 1, p).wait_recv()
            if relay:
                for p in range(2):
                    second_phase(t - 1, p).start()

        @pl.when(t >= 2)
        def _():
            c = t - 2
            if relay:
                for p in range(2):
                    second_arrival(c, p).wait_recv()
            acc[c] = jnp.zeros_like(acc[c])
            compute(c)
            service(c + 1)

    @pl.loop(0, ny)
    def _(y):
        for x in range(nx):
            save(x, y).wait()
            give(x, y).wait()

        @pl.when(has_hi)
        def _():
            halo_up(y).wait_send()

        @pl.when(has_lo)
        def _():
            halo_dn(y).wait_send()

        for p in range(len(partners)):
            first_phase(y, p).wait_send()
        if relay:
            for p in range(2):
                second_phase(y, p).wait_send()

    @pl.when(has_hi)
    def _():
        lim_up.wait_send()

    @pl.when(has_lo)
    def _():
        lim_dn.wait_send()

    @pl.loop(0, groups)
    def _(g):
        h, i = g // nsl, g % nsl
        for way in range(2):
            @pl.when(sends(way, h))
            def _():
                onward(way, h, i).wait_send()

            here = held(way, h) if way == 0 else jnp.logical_and(h > 0, held(way, h))

            @pl.when(here)
            def _():
                across(way, h, i).wait_send()


def local(nv, ns, density, limiter, heading, courant, kernel_slices):
    vl, nx, ny, lanes = density.shape
    nsl, vels, _ = kernel_slices.shape
    rows = nx * ny
    nz = ns // 2
    bf16, f32 = jnp.bfloat16, jnp.float32
    dens = density.reshape(vl, rows, 1, lanes)
    lim = limiter.reshape(rows, lanes)
    signed = jnp.where(heading == 1, courant, -courant)
    signed = jnp.broadcast_to(signed[:, None], (vl, lanes))
    dma = pltpu.SemaphoreType.DMA
    n_part = 2 if nv == 4 else max(nv - 1, 1)
    vmem = pl.BlockSpec(memory_space=pltpu.VMEM)
    out = jax.ShapeDtypeStruct(dens.shape, f32)
    hbm = pl.BlockSpec(memory_space=pl.ANY)
    trans, coll = pl.pallas_call(
        functools.partial(kernel, nv, ns, nx, ny, vl, nsl),
        out_shape=(out, out),
        in_specs=[hbm, vmem, vmem, vmem],
        out_specs=(hbm, hbm),
        scratch_shapes=[
            pltpu.VMEM((ny, vl, nx * lanes), f32),
            pltpu.VMEM((ny, vels, nx * lanes), bf16),
            pltpu.VMEM((nsl * ns, vl, vels), bf16),
            pltpu.VMEM((ny, 2, vl, lanes), bf16),
            pltpu.VMEM((ny, 2, vl, lanes), bf16),
            pltpu.VMEM((ny, 2, vl, lanes), bf16),
            pltpu.VMEM((ny, 2, vl, lanes), bf16),
            pltpu.VMEM((ny, lanes), jnp.int32),
            pltpu.VMEM((ny, lanes), jnp.int32),
            pltpu.VMEM((ny, nx, vl, lanes), f32),
            dma((ny, nx)), dma((ny, nx)), dma((ny, nx)),
            dma((2, ny)), dma((2, ny)), dma((2,)), dma((2,)),
            dma((n_part, ny)), dma((n_part, ny)), dma((2, ny)), dma((2, ny)),
            dma((2, nz, nsl)), dma((2, nz, nsl)), dma((2, nz, nsl)), dma((2, nz, nsl)),
        ],
        compiler_params=pltpu.CompilerParams(
            collective_id=0, has_side_effects=True, vmem_limit_bytes=60 * 1024 * 1024
        ),
    )(dens, lim, signed, kernel_slices)
    return trans.reshape(density.shape), coll.reshape(density.shape)


def solution(mesh):
    return jax.shard_map(
        functools.partial(local, mesh.shape["vel"], mesh.shape["space"]),
        mesh=mesh,
        in_specs=(
            P("vel", "space", None, None),
            P("space", None, None),
            P("vel"),
            P("vel"),
            P("space", None, "vel"),
        ),
        out_specs=(P("vel", "space", None, None), P("vel", "space", None, None)),
        check_vma=False,
    )
```

```python
import functools

import jax
import jax.numpy as jnp
from jax import lax
from jax.experimental import pallas as pl
from jax.experimental.pallas import tpu as pltpu
from jax.sharding import PartitionSpec as P

MESH = pl.DeviceIdType.MESH


def minmod(left, right):
    small = jnp.where(left > 0, jnp.minimum(left, right), jnp.maximum(left, right))
    return jnp.where(left * right > 0, small, jnp.zeros_like(left))


def kernel(
    nv, ns, nx, ny, vl, nsl,
    dens_ref, lim_ref, vel_ref, ker_ref,
    trans_ref, coll_ref,
    acc, gath, kt, send_up, send_dn, recv_lo, recv_hi, lim_lo, lim_hi,
    dbuf, in_s, trans_s, coll_s,
    halo_s, halo_r, lim_s, lim_r, v1_s, v1_r, v2_s, v2_r, k_s, k_r, c_s, c_r,
):
    vels = nv * vl
    lanes = dens_ref.shape[3]
    stride = vels // (nsl * ns)
    half = vl // 2
    v = lax.axis_index("vel")
    sp = lax.axis_index("space")
    nz = ns // 2
    z = sp // 2
    core = sp % 2
    relay = nv == 4
    if relay:
        partners = [v + 1 - 2 * (v % 2), v + 2 - 4 * ((v // 2) % 2)]
        sources = partners
    else:
        partners = [(v + p) % nv for p in range(1, nv)]
        sources = [(v + nv - p) % nv for p in range(1, nv)]
    sibling = 2 * z + 1 - core
    z_up = 2 * ((z + 1) % nz) + core
    z_dn = 2 * ((z + nz - 1) % nz) + core
    s_up = (sp + 1) % ns
    s_dn = (sp + ns - 1) % ns
    has_lo = sp > 0
    has_hi = sp < ns - 1
    groups = nz * nsl

    def load(x, y):
        return pltpu.make_async_copy(dens_ref.at[:, x * ny + y, 0, :], dbuf.at[y, x], in_s.at[y, x])

    def save(x, y):
        return pltpu.make_async_copy(dbuf.at[y, x], trans_ref.at[:, x * ny + y, 0, :], trans_s.at[y, x])

    def give(x, y):
        tile = acc.at[y, :, pl.ds(x * lanes, lanes)]
        return pltpu.make_async_copy(tile, coll_ref.at[:, x * ny + y, 0, :], coll_s.at[y, x])

    @pl.loop(0, ny)
    def _(y):
        for x in range(nx):
            load(x, y).start()

    barrier = pltpu.get_barrier_semaphore()
    for p in partners:
        pl.semaphore_signal(barrier, inc=1, device_id={"vel": p}, device_id_type=MESH)
    for p in (sibling, z_up, z_dn, s_up, s_dn):
        pl.semaphore_signal(barrier, inc=1, device_id={"space": p}, device_id_type=MESH)
    pl.semaphore_wait(barrier, len(partners) + 5)

    def remote(src, dst, ss, rs, axis, peer):
        return pltpu.make_async_remote_copy(
            src_ref=src, dst_ref=dst, send_sem=ss, recv_sem=rs,
            device_id={axis: peer}, device_id_type=MESH,
        )

    def halo_up(y):
        return remote(send_up.at[y], recv_lo.at[y], halo_s.at[0, y], halo_r.at[0, y], "space", s_up)

    def halo_dn(y):
        return remote(send_dn.at[y], recv_hi.at[y], halo_s.at[1, y], halo_r.at[1, y], "space", s_dn)

    lim_up = remote(lim_ref.at[pl.ds((nx - 1) * ny, ny)], lim_lo, lim_s.at[0], lim_r.at[0], "space", s_up)
    lim_dn = remote(lim_ref.at[pl.ds(0, ny)], lim_hi, lim_s.at[1], lim_r.at[1], "space", s_dn)

    @pl.when(has_hi)
    def _():
        lim_up.start()

    @pl.when(has_lo)
    def _():
        lim_dn.start()

    blk = min(256, vels)

    def chip_at(way, h):
        return z - h if way == 0 else z + h

    def held(way, h):
        return z - h >= 0 if way == 0 else z + h < nz

    def slice_of(way, h, i, c):
        return kt.at[pl.ds((2 * chip_at(way, h) + c) * nsl + i, 1)]

    def onward(way, h, i):
        piece = slice_of(way, h, i, core)
        return remote(piece, piece, k_s.at[way, h, i], k_r.at[way, h, i], "space", (z_up, z_dn)[way])

    def sends(way, h):
        more = z < nz - 1 if way == 0 else z > 0
        return jnp.logical_and(more, held(way, h))

    def arrival(way, h, i):
        piece = slice_of(way, h, i, core)
        return remote(piece, piece, k_s.at[way, h - 1, i], k_r.at[way, h - 1, i], "space", (z_up, z_dn)[way])

    def across(way, h, i):
        piece = slice_of(way, h, i, core)
        return remote(piece, piece, c_s.at[way, h, i], c_r.at[way, h, i], "space", sibling)

    def from_sibling(way, h, i):
        piece = slice_of(way, h, i, 1 - core)
        return remote(piece, piece, c_s.at[way, h, i], c_r.at[way, h, i], "space", sibling)

    @pl.loop(0, nsl)
    def _(i):
        for j in range(0, vels, blk):
            kt[sp * nsl + i, :, j : j + blk] = ker_ref[i, j : j + blk, :].T

    @pl.loop(0, ny)
    def _(y):
        for x in range(nx):
            load(x, y).wait()
        send_up[y, 0] = dbuf[y, nx - 1].astype(jnp.bfloat16)
        send_up[y, 1] = dbuf[y, nx - 2].astype(jnp.bfloat16)
        send_dn[y, 0] = dbuf[y, 0].astype(jnp.bfloat16)
        send_dn[y, 1] = dbuf[y, 1].astype(jnp.bfloat16)

        @pl.when(has_hi)
        def _():
            halo_up(y).start()

        @pl.when(has_lo)
        def _():
            halo_dn(y).start()

    @pl.loop(0, nsl)
    def _(i):
        for way in range(2):
            @pl.when(sends(way, 0))
            def _():
                onward(way, 0, i).start()
        across(0, 0, i).start()

    @pl.when(has_lo)
    def _():
        lim_up.wait_recv()

    @pl.when(has_hi)
    def _():
        lim_dn.wait_recv()

    @pl.when(jnp.logical_not(has_lo))
    def _():
        lim_lo[...] = jnp.zeros_like(lim_lo)
        recv_lo[...] = jnp.zeros_like(recv_lo)

    @pl.when(jnp.logical_not(has_hi))
    def _():
        lim_hi[...] = jnp.zeros_like(lim_hi)
        recv_hi[...] = jnp.zeros_like(recv_hi)

    def slope(left, right, code):
        central = 0.5 * (left + right)
        return jnp.where(
            code == 1, minmod(left, right), jnp.where(code == 2, central, jnp.zeros_like(central))
        )

    rb = 32

    def transport(y):
        @pl.loop(0, vl // rb)
        def _(b):
            r0 = pl.multiple_of(b * rb, rb)
            signed = vel_ref[pl.ds(r0, rb), :]
            forward = signed > 0
            cour = jnp.abs(signed)
            upw = jnp.where(forward, jnp.float32(0.5), jnp.float32(-0.5))
            d = [recv_lo[y, 1, pl.ds(r0, rb), :].astype(jnp.float32),
                 recv_lo[y, 0, pl.ds(r0, rb), :].astype(jnp.float32)]
            d += [dbuf[y, x, pl.ds(r0, rb), :] for x in range(nx)]
            d += [recv_hi[y, 0, pl.ds(r0, rb), :].astype(jnp.float32),
                  recv_hi[y, 1, pl.ds(r0, rb), :].astype(jnp.float32)]
            codes = [lim_lo[pl.ds(y, 1), :]]
            codes += [lim_ref[pl.ds(x * ny + y, 1), :] for x in range(nx)]
            codes += [lim_hi[pl.ds(y, 1), :]]
            diff = [d[i + 1] - d[i] for i in range(nx + 3)]
            r = []
            for i in range(nx + 2):
                code = jnp.broadcast_to(codes[i], (rb, lanes))
                r.append(d[i + 1] + upw * slope(diff[i], diff[i + 1], code))
            for x in range(nx):
                upstream = jnp.where(forward, r[x], r[x + 2])
                out = d[x + 2] - cour * (r[x + 1] - upstream)
                dbuf[y, x, pl.ds(r0, rb), :] = out
                gath[y, pl.ds(pl.multiple_of(v * vl + r0, rb), rb), x * lanes : (x + 1) * lanes] = (
                    out.astype(jnp.bfloat16)
                )

    def mine(y, owner):
        return gath.at[y, pl.ds(pl.multiple_of(owner * vl, vl), vl)]

    def first_phase(y, p):
        return remote(mine(y, v), mine(y, v), v1_s.at[p, y], v1_r.at[p, y], "vel", partners[p])

    def first_arrival(y, p):
        piece = mine(y, sources[p])
        return remote(piece, piece, v1_s.at[p, y], v1_r.at[p, y], "vel", partners[p])

    def part(y, owner, which):
        return gath.at[y, pl.ds(pl.multiple_of(owner * vl + which * half, half), half)]

    def second_phase(y, p):
        piece = part(y, partners[1 - p], p)
        return remote(piece, piece, v2_s.at[p, y], v2_r.at[p, y], "vel", partners[p])

    def second_arrival(y, p):
        far = partners[0] + partners[1] - v
        piece = part(y, far, p)
        return remote(piece, piece, v2_s.at[p, y], v2_r.at[p, y], "vel", partners[p])

    def one(c, chip, i):
        total = acc[c]
        for k in range(2):
            s = (2 * chip + k) * nsl + i
            prod = jnp.dot(kt[s], gath[c], preferred_element_type=jnp.float32)
            row = gath[c, pl.ds(pl.multiple_of(s * stride, stride), 1), :].astype(jnp.float32)
            total = total + row * prod
        acc[c] = total

    def first_chunk(g):
        later = jnp.clip((g * ny) // groups, 1, ny - 1)
        return jnp.where(g < nsl, 0, later)

    def compute(c):
        @pl.loop(0, groups)
        def _(g):
            h, i = g // nsl, g % nsl
            start = first_chunk(g)
            early = jnp.where(c < start, c + 1, jnp.where(c == start, 0, c))
            for way in range(2):
                here = held(way, h) if way == 0 else jnp.logical_and(h > 0, held(way, h))

                @pl.when(jnp.logical_and(here, c == start))
                def _():
                    from_sibling(way, h, i).wait_recv()

            @pl.loop(early, c + 1)
            def _(cc):
                low = jnp.where(z - h >= 0, 0, 1)
                high = jnp.where(jnp.logical_and(h > 0, z + h < nz), 2, 1)

                @pl.loop(low, high)
                def _(way):
                    one(cc, z + (2 * way - 1) * h, i)

                @pl.when(jnp.logical_and(g == groups - 1, c >= start))
                def _():
                    for x in range(nx):
                        give(x, cc).start()

    def service(c):
        @pl.loop(nsl, groups)
        def _(g):
            h, i = g // nsl, g % nsl

            @pl.when(first_chunk(g) == c)
            def _():
                for way in range(2):
                    @pl.when(held(way, h))
                    def _():
                        arrival(way, h, i).wait_recv()

                        @pl.when(sends(way, h))
                        def _():
                            onward(way, h, i).start()

                        across(way, h, i).start()

    @pl.loop(0, ny + 2)
    def _(t):
        @pl.when(t < ny)
        def _():
            @pl.when(has_lo)
            def _():
                halo_up(t).wait_recv()

            @pl.when(has_hi)
            def _():
                halo_dn(t).wait_recv()

            transport(t)
            for p in range(len(partners)):
                first_phase(t, p).start()
            for x in range(nx):
                save(x, t).start()

        @pl.when(jnp.logical_and(t >= 1, t < ny + 1))
        def _():
            for p in range(len(partners)):
                first_arrival(t - 1, p).wait_recv()
            if relay:
                for p in range(2):
                    second_phase(t - 1, p).start()

        @pl.when(t >= 2)
        def _():
            c = t - 2
            if relay:
                for p in range(2):
                    second_arrival(c, p).wait_recv()
            acc[c] = jnp.zeros_like(acc[c])
            compute(c)
            service(c + 1)

    @pl.loop(0, ny)
    def _(y):
        for x in range(nx):
            save(x, y).wait()
            give(x, y).wait()

        @pl.when(has_hi)
        def _():
            halo_up(y).wait_send()

        @pl.when(has_lo)
        def _():
            halo_dn(y).wait_send()

        for p in range(len(partners)):
            first_phase(y, p).wait_send()
        if relay:
            for p in range(2):
                second_phase(y, p).wait_send()

    @pl.when(has_hi)
    def _():
        lim_up.wait_send()

    @pl.when(has_lo)
    def _():
        lim_dn.wait_send()

    @pl.loop(0, groups)
    def _(g):
        h, i = g // nsl, g % nsl
        for way in range(2):
            @pl.when(sends(way, h))
            def _():
                onward(way, h, i).wait_send()

            here = held(way, h) if way == 0 else jnp.logical_and(h > 0, held(way, h))

            @pl.when(here)
            def _():
                across(way, h, i).wait_send()


def local(nv, ns, density, limiter, heading, courant, kernel_slices):
    vl, nx, ny, lanes = density.shape
    nsl, vels, _ = kernel_slices.shape
    rows = nx * ny
    nz = ns // 2
    bf16, f32 = jnp.bfloat16, jnp.float32
    dens = density.reshape(vl, rows, 1, lanes)
    lim = limiter.reshape(rows, lanes)
    signed = jnp.where(heading == 1, courant, -courant)
    signed = jnp.broadcast_to(signed[:, None], (vl, lanes))
    dma = pltpu.SemaphoreType.DMA
    n_part = 2 if nv == 4 else max(nv - 1, 1)
    vmem = pl.BlockSpec(memory_space=pltpu.VMEM)
    out = jax.ShapeDtypeStruct(dens.shape, f32)
    hbm = pl.BlockSpec(memory_space=pl.ANY)
    trans, coll = pl.pallas_call(
        functools.partial(kernel, nv, ns, nx, ny, vl, nsl),
        out_shape=(out, out),
        in_specs=[hbm, vmem, vmem, vmem],
        out_specs=(hbm, hbm),
        scratch_shapes=[
            pltpu.VMEM((ny, vl, nx * lanes), f32),
            pltpu.VMEM((ny, vels, nx * lanes), bf16),
            pltpu.VMEM((nsl * ns, vl, vels), bf16),
            pltpu.VMEM((ny, 2, vl, lanes), bf16),
            pltpu.VMEM((ny, 2, vl, lanes), bf16),
            pltpu.VMEM((ny, 2, vl, lanes), bf16),
            pltpu.VMEM((ny, 2, vl, lanes), bf16),
            pltpu.VMEM((ny, lanes), jnp.int32),
            pltpu.VMEM((ny, lanes), jnp.int32),
            pltpu.VMEM((ny, nx, vl, lanes), f32),
            dma((ny, nx)), dma((ny, nx)), dma((ny, nx)),
            dma((2, ny)), dma((2, ny)), dma((2,)), dma((2,)),
            dma((n_part, ny)), dma((n_part, ny)), dma((2, ny)), dma((2, ny)),
            dma((2, nz, nsl)), dma((2, nz, nsl)), dma((2, nz, nsl)), dma((2, nz, nsl)),
        ],
        compiler_params=pltpu.CompilerParams(
            collective_id=0, has_side_effects=True, vmem_limit_bytes=60 * 1024 * 1024
        ),
    )(dens, lim, signed, kernel_slices)
    return trans.reshape(density.shape), coll.reshape(density.shape)


def solution(mesh):
    return jax.shard_map(
        functools.partial(local, mesh.shape["vel"], mesh.shape["space"]),
        mesh=mesh,
        in_specs=(
            P("vel", "space", None, None),
            P("space", None, None),
            P("vel"),
            P("vel"),
            P("space", None, "vel"),
        ),
        out_specs=(P("vel", "space", None, None), P("vel", "space", None, None)),
        check_vma=False,
    )
```
